128 devices in a mesh: row: 8 (over y, z_lo), col: 16 (over x, z_hi, core).
Axes of the slice: x: 4, y: 4, z: 4 (z_hi: 2, z_lo: 2; z = z_hi * 2 + z_lo), core: 2. Of those that a mesh axis runs over, the one named last changes fastest.
Arguments:
- spectra: bfloat16 [4096, 8, 1536], P(('row', 'col')), may hold values from -6 to 6
- pair_bins: int32 [4, 4096, 32], P(None, ('row', 'col')), may hold values from 0 to 127
- dead_mask: int32 [4096], P(('row', 'col')), may hold values 0 or 1
Outputs:
- stacked_lags: float32 [128, 896], P(('row', 'col'))
The draws below stay inside these ranges and needn't reach their ends.
All inputs are finite; a program needn't handle non-finite values. No bound on the sum of `dead_mask` on one device may be relied on, other than what follows from the above.
Results may differ from the reference program's by a relative error of at most 0.0041.
Values may be sent and summed in bfloat16 or wider, within the bound.
A program may use at most 256 MiB of HBM per device.

```python
import math
import jax
import jax.numpy as jnp
from jax import lax

CB = 32
W = 8
F = 768
NT = 1600
LAGS = 896
NB = 128
ROUNDS = 4
CHANNELS = 4096
N_ROW = 8
N_COL = 16


def with_ends(entries, rng, smallest, high):
    extent = entries.shape
    index_at = [jax.random.randint(jax.random.fold_in(rng, axis), (), 0, extent[axis]) for axis in range(len(extent))]
    entries = entries.at[tuple(index_at)].set(smallest)
    longest = extent.index(max(extent))
    index_at[longest] = (index_at[longest] + 1) % extent[longest]
    return entries.at[tuple(index_at)].set(high)


def steps_of(rng, extent, split, low, largest):
    def one(axis_at, parts):
        draws = jax.random.uniform(jax.random.fold_in(jax.random.fold_in(rng, 6), axis_at), (parts,), jnp.float32, low / len(split), largest / len(split))
        return jnp.repeat(jnp.exp(draws), extent[axis_at] // parts).reshape((-1,) + (1,) * (len(extent) - axis_at - 1))

    loudness = one(*split[0])
    for cut in split[1:]:
        loudness = loudness * one(*cut)
    return loudness


def noise(rng, shape, deviation, limit, pieces=(), held_as=jnp.bfloat16):
    level = steps_of(rng, shape, pieces, -0.22, 0.18) if pieces else 1.0
    array = jax.random.normal(rng, shape, jnp.float32) * deviation * level
    return jnp.minimum(jnp.maximum(array, -limit), limit).astype(held_as)


def setup_inputs(seed: int = 0) -> dict:
    splits = jax.random.split(jax.random.key(seed), 4)
    return {
        "spectra": noise(splits[0], (CHANNELS, W, 2 * F), 1.0, 6.0, ((0, 128),)),
        "pair_bins": with_ends(jax.random.randint(splits[1], (ROUNDS, CHANNELS, CB), 0, NB), jax.random.fold_in(splits[1], 1), 0, NB - 1).astype(jnp.int32),
        "dead_mask": with_ends((jax.random.randint(splits[2], (CHANNELS,), 0, 8) < 7).astype(jnp.int32), jax.random.fold_in(splits[2], 1), 0, 1),
    }


def whiten(spectra, dead_mask):
    values = spectra.astype(jnp.float32)
    powers = lax.optimization_barrier(jnp.mean(values * values, axis=-1, keepdims=True))
    alive = dead_mask.astype(jnp.float32)[:, None, None]
    return (values / jnp.sqrt(powers + 1e-06) * alive).astype(jnp.bfloat16)

def cross_spectra(local_part, remote_part):
    half_len = local_part.shape[-1] // 2
    first = local_part.astype(jnp.float32)
    second = remote_part.astype(jnp.float32)
    high = lax.Precision.HIGHEST
    one_real, one_imag = (first[..., :half_len], first[..., half_len:])
    two_real, two_imag = (second[..., :half_len], second[..., half_len:])
    real_part = jnp.einsum('iwk,jwk->ijk', one_real, two_real, precision=high) + jnp.einsum('iwk,jwk->ijk', one_imag, two_imag, precision=high)
    imag_part = jnp.einsum('iwk,jwk->ijk', one_imag, two_real, precision=high) - jnp.einsum('iwk,jwk->ijk', one_real, two_imag, precision=high)
    channels = local_part.shape[0]
    return jnp.concatenate([real_part, imag_part], axis=-1).reshape(channels * remote_part.shape[0], 2 * half_len)

def build_table(freq_len, lag_len, length):
    freq_ids = jnp.arange(freq_len, dtype=jnp.int32)
    lag_ids = jnp.arange(lag_len, dtype=jnp.int32) - lag_len // 2
    phases = freq_ids[:, None] * lag_ids[None, :] % length
    angles = phases.astype(jnp.float32) * (2.0 * math.pi / length)
    weights = jnp.where(freq_ids == 0, 1.0, 2.0).astype(jnp.float32)[:, None]
    return jnp.concatenate([weights * jnp.cos(angles), -weights * jnp.sin(angles)], axis=0)

def reference(spectra, pair_bins, dead_mask):
    whitened = whiten(spectra, dead_mask)
    groups = N_ROW * N_COL
    block_size = spectra.shape[0] // groups
    freq_len = spectra.shape[2] // 2
    width = spectra.shape[1]

    def step_fn(stacked, position):
        round_no = position // groups
        device = position % groups
        partner = jnp.bitwise_xor(device, jnp.left_shift(jnp.int32(1), round_no)).astype(jnp.int32)
        local_part = lax.dynamic_slice_in_dim(whitened, (device * block_size).astype(jnp.int32), block_size, 0)
        remote_part = lax.dynamic_slice_in_dim(whitened, (partner * block_size).astype(jnp.int32), block_size, 0)
        bin_ids = lax.dynamic_slice(pair_bins, (round_no.astype(jnp.int32), (device * block_size).astype(jnp.int32), jnp.int32(0)), (1, block_size, block_size)).reshape(-1)
        stacked = stacked + jax.ops.segment_sum(cross_spectra(local_part, remote_part), bin_ids, num_segments=NB)
        return (stacked, None)
    start = jnp.zeros((NB, 2 * freq_len), jnp.float32)
    stacked, _ = lax.scan(step_fn, start, jnp.arange(ROUNDS * groups, dtype=jnp.int32))
    pairs = ROUNDS * block_size * block_size * groups // NB
    scaling = 1.0 / (2.0 * math.sqrt(freq_len * width * pairs))
    table = build_table(freq_len, LAGS, NT)
    return jnp.dot(stacked, table, precision=lax.Precision.HIGHEST) * scaling
```

```python
import functools
import math

import jax
import jax.numpy as jnp
import numpy as np
from jax import lax
from jax.experimental import pallas as pl
from jax.experimental.pallas import tpu as pltpu
from jax.sharding import PartitionSpec as P

NT = 1600
LAGS = 896
NB = 128
ROUNDS = 4
CB = 32
W = 8
F = 768
N_ROW = 8
N_COL = 16
FC = 16
HALF = F // 2
CHUNKS = HALF // FC
PIECES = 6
CP = CHUNKS // PIECES
MESH = pl.DeviceIdType.MESH
F32 = jnp.float32
BF16 = jnp.bfloat16


def tables():
    at = np.arange(F, dtype=np.int64)
    k = at // 128 * 128 + -(at % 128 // FC) % 8 * FC + at % FC
    scale = 1.0 / (2.0 * math.sqrt(F * W * (ROUNDS * CB * CB * N_ROW * N_COL // NB)))
    weight = np.where(k == 0, 1.0, 2.0) * scale
    start = 128 * np.arange(8, dtype=np.int64) - LAGS // 2
    first = (start[:, None] * k[None, :] % NT) * (2.0 * np.pi / NT)
    cos1 = (np.cos(first) * weight).reshape(8, 2, HALF).transpose(1, 0, 2)
    sin1 = (np.sin(first) * weight).reshape(8, 2, HALF).transpose(1, 0, 2)
    e1 = np.stack([cos1, sin1], axis=1).astype(np.float32)
    second = (k[:, None] * np.arange(128, dtype=np.int64)[None, :] % NT) * (2.0 * np.pi / NT)
    cos2 = np.cos(second).reshape(2, HALF, 128)
    sin2 = -np.sin(second).reshape(2, HALF, 128)
    e2 = np.concatenate([cos2, sin2], axis=1).astype(np.float32)
    high = e2.astype(jnp.bfloat16)
    low = (e2 - high.astype(np.float32)).astype(jnp.bfloat16)
    return e1, np.stack([high, low], axis=0)


def flip(value, mask):
    for bit in range(4):
        if mask >> bit & 1:
            value = value + (1 << bit) * (1 - 2 * ((value // (1 << bit)) % 2))
    return value


def nt_dot(a, b):
    return lax.dot_general(a, b, (((1,), (1,)), ((), ())), preferred_element_type=F32)


def kernel(
    alive_ref, spec_hbm, bins_ref, e1_hbm, e2_hbm, out_ref,
    x_v, d_v, send_v, recv_v, relay_v, pbs_v, pbr_v, oh_v, cross_v, part_v, rows_v, s2_v, r2_v, e1_v, e2_v,
    local_sem, pb_ss, pb_rs, a_ss, a_rs, f_ss, f_rs, row_ss, row_rs, col_ss, col_rs,
):
    row = lax.axis_index("row")
    col = lax.axis_index("col")
    parity = (col + col // 2 + col // 4 + col // 8) % 2

    def device(mask):
        return (flip(row, mask >> 4), flip(col, mask & 15))

    load = pltpu.make_async_copy(spec_hbm, x_v, local_sem.at[0])
    load.start()
    load_e1 = pltpu.make_async_copy(e1_hbm, e1_v, local_sem.at[1])
    load_e1.start()
    load_e2 = pltpu.make_async_copy(e2_hbm, e2_v, local_sem.at[2])
    load_e2.start()

    peers = sorted({16 * k for k in range(1, 8)} | set(range(1, 16)) | {18})
    barrier = pltpu.get_barrier_semaphore()
    for mask in peers:
        pl.semaphore_signal(barrier, inc=1, device_id=device(mask), device_id_type=MESH)

    bins = bins_ref[...].reshape(ROUNDS * CB, CB)
    padded = jnp.concatenate([bins, jnp.zeros((128, 96), jnp.int32)], axis=1).astype(F32)
    pbs_v[...] = padded.T[:CB, :].astype(jnp.int32)
    load.wait()

    lane = lax.broadcasted_iota(jnp.int32, (8, 128), 1) // 16
    bits = [(lane // (1 << s)) % 2 == 1 for s in range(3)]

    def whiten(i, _):
        x = x_v[i].astype(F32)
        power = jnp.mean(x * x, axis=-1, keepdims=True)
        alive = alive_ref[i].astype(F32)
        y = x * (alive / jnp.sqrt(power + 1e-06))
        for c in range(2):
            for ft in range(6):
                t = y[:, c * F + ft * 128 : c * F + ft * 128 + 128]
                t = pltpu.roll(t, 0, 1, stride=16, stride_axis=0)
                for s in range(3):
                    t = jnp.where(bits[s], pltpu.roll(t, 8 - (1 << s), 0), t)
                d_v[c, pl.ds(ft * 8 * CB + i, 8, stride=CB), :] = t
        return 0

    lax.fori_loop(0, CB, whiten, 0)

    def pack(q, _):
        start = pl.multiple_of(((1 - parity) * CHUNKS + q) * CB, CB)
        for c in range(2):
            send_v[q, :, c * 128 : c * 128 + 128] = d_v[c, pl.ds(start, CB), :].astype(BF16)
        return 0

    lax.fori_loop(0, CHUNKS, pack, 0)

    pl.semaphore_wait(barrier, len(peers))

    bin_copies = [
        pltpu.make_async_remote_copy(
            src_ref=pbs_v, dst_ref=pbr_v.at[r], send_sem=pb_ss.at[r], recv_sem=pb_rs.at[r],
            device_id=device(1 << r), device_id_type=MESH)
        for r in range(ROUNDS)
    ]
    for copy in bin_copies:
        copy.start()

    def span(piece):
        return pl.ds(piece * CP, CP)

    def core_copy(piece):
        return pltpu.make_async_remote_copy(
            src_ref=send_v.at[span(piece)], dst_ref=recv_v.at[0, span(piece)],
            send_sem=a_ss.at[0, piece], recv_sem=a_rs.at[0, piece], device_id=device(1), device_id_type=MESH)

    def x_copy(piece):
        return pltpu.make_async_remote_copy(
            src_ref=send_v.at[span(piece)], dst_ref=recv_v.at[2, span(piece)],
            send_sem=a_ss.at[1, piece], recv_sem=a_rs.at[1, piece], device_id=device(4), device_id_type=MESH)

    def z_device(odd):
        return (flip(row, 1), col + odd * (flip(col, 2) - col))

    def z_copy(piece):
        return pltpu.make_async_remote_copy(
            src_ref=send_v.at[span(piece)], dst_ref=relay_v.at[span(piece)],
            send_sem=a_ss.at[2, piece], recv_sem=a_rs.at[2, piece],
            device_id=z_device(piece % 2), device_id_type=MESH)

    def x_forward(piece):
        return pltpu.make_async_remote_copy(
            src_ref=recv_v.at[2, span(piece)], dst_ref=recv_v.at[3, span(piece)],
            send_sem=f_ss.at[0, piece], recv_sem=f_rs.at[0, piece], device_id=device(12), device_id_type=MESH)

    def z_forward(piece):
        return pltpu.make_async_remote_copy(
            src_ref=relay_v.at[span(piece)], dst_ref=recv_v.at[1, span(piece)],
            send_sem=f_ss.at[1, piece], recv_sem=f_rs.at[1, piece],
            device_id=z_device(1 - piece % 2), device_id_type=MESH)

    def send(piece, _):
        x_copy(piece).start()
        z_copy(piece).start()
        core_copy(piece).start()
        return 0

    lax.fori_loop(0, PIECES, send, 0)

    for copy in bin_copies:
        copy.wait()
    own = jnp.concatenate([bins_ref[r] for r in range(ROUNDS)], axis=1)
    of_round = lax.broadcasted_iota(jnp.int32, (CB, 128), 1) // CB
    other = pbr_v[0]
    for r in range(1, ROUNDS):
        other = jnp.where(of_round == r, pbr_v[r], other)
    bin_ids = lax.broadcasted_iota(jnp.int32, (NB, 128), 0)
    for i in range(CB):
        one = (own[i : i + 1, :] == bin_ids).astype(F32)
        two = (other[i : i + 1, :] == bin_ids).astype(F32)
        oh_v[0, :, i * 128 : i * 128 + 128] = (one + two).astype(BF16)
        oh_v[1, :, i * 128 : i * 128 + 128] = (one - two).astype(BF16)

    mask = (
        lax.broadcasted_iota(jnp.int32, (FC, 256), 1) % FC == lax.broadcasted_iota(jnp.int32, (FC, 256), 0)
    ).astype(F32).astype(BF16)

    def products(q, _):
        start = (parity * CHUNKS + q) * CB
        parts = []
        for i in range(CB):
            v = [d_v[c, pl.ds(start + i, 8, stride=0), :] for c in range(2)]
            v = jnp.concatenate([jnp.concatenate([u, u], axis=0).astype(BF16) for u in v], axis=1)
            parts.append(v * mask)
        lhs = jnp.concatenate(parts, axis=0)
        other_part = recv_v[:, q].reshape(ROUNDS * CB, 256)
        turned = jnp.concatenate([-other_part[:, 128:], other_part[:, :128]], axis=1)
        rhs = jnp.concatenate([other_part, turned], axis=0)
        cross = nt_dot(lhs, rhs).astype(BF16)
        cross_v[:, pl.ds(pl.multiple_of(q * FC, FC), FC), :] = cross.reshape(CB, FC, 256)
        return 0

    def step(piece, _):
        @pl.when(piece < PIECES)
        def _():
            x_copy(piece).wait_recv()
            x_forward(piece).start()
            z_copy(piece).wait_recv()
            z_forward(piece).start()

        @pl.when(piece >= 1)
        def _():
            before = piece - 1
            core_copy(before).wait_recv()
            x_forward(before).wait_recv()
            z_forward(before).wait_recv()
            lax.fori_loop(before * CP, before * CP + CP, products, 0)
        return 0

    lax.fori_loop(0, PIECES + 1, step, 0)

    for c in range(2):
        for ft in range(HALF // 128):
            values = jnp.concatenate(
                [cross_v[i, ft * 128 : ft * 128 + 128, c * 128 : c * 128 + 128] for i in range(CB)], axis=1)
            total = nt_dot(oh_v[c], values)
            at = c * HALF + ft * 128
            part_v[:, :, at : at + 128] = total.astype(BF16).reshape(N_ROW, NB // N_ROW, 128)

    row_copies = [
        pltpu.make_async_remote_copy(
            src_ref=part_v.at[flip(row, k)], dst_ref=rows_v.at[k - 1],
            send_sem=row_ss.at[k - 1], recv_sem=row_rs.at[k - 1], device_id=device(16 * k), device_id_type=MESH)
        for k in range(1, N_ROW)
    ]
    for copy in row_copies:
        copy.start()
    total = part_v[row].astype(F32)
    for k, copy in enumerate(row_copies):
        copy.wait_recv()
        total = total + rows_v[k].astype(F32)
    for k in range(6):
        s2_v[pl.ds(k, N_COL, stride=8), :] = total[:, k * 128 : k * 128 + 128]

    col_copies = [
        pltpu.make_async_remote_copy(
            src_ref=s2_v.at[pl.ds(pl.multiple_of(flip(col, k) * 8, 8), 8), :], dst_ref=r2_v.at[k - 1],
            send_sem=col_ss.at[k - 1], recv_sem=col_rs.at[k - 1], device_id=device(k), device_id_type=MESH)
        for k in range(1, N_COL)
    ]
    for copy in col_copies:
        copy.start()
    load_e1.wait()
    load_e2.wait()
    sums = [s2_v[pl.ds(pl.multiple_of(col * 8, 8), 8), :], None]
    for k, copy in enumerate(col_copies, 1):
        copy.wait_recv()
        odd = bin(k).count("1") % 2
        sums[odd] = r2_v[k - 1] if sums[odd] is None else sums[odd] + r2_v[k - 1]

    result = None
    for which in range(2):
        half = parity if which == 0 else 1 - parity
        x = sums[which]
        reals, imags = [], []
        for ft in range(3):
            cos1 = e1_v[half, 0, :, ft * 128 : ft * 128 + 128]
            sin1 = e1_v[half, 1, :, ft * 128 : ft * 128 + 128]
            re, im = x[ft : ft + 1, :], x[3 + ft : 4 + ft, :]
            reals.append(re * cos1 - im * sin1)
            imags.append(re * sin1 + im * cos1)
        turned = jnp.concatenate(reals + imags, axis=1)
        high = turned.astype(BF16)
        low = (turned - high.astype(F32)).astype(BF16)
        both = jnp.concatenate([high, low], axis=0)
        for part in range(2):
            o = jnp.dot(both, e2_v[part, half], preferred_element_type=F32)
            o = o[:8] + o[8:]
            result = o if result is None else result + o
    for mh in range(LAGS // 128):
        out_ref[0:1, mh * 128 : mh * 128 + 128] = result[mh : mh + 1, :]

    for copy in row_copies + col_copies:
        copy.wait_send()

    def drain(piece, _):
        for make in (core_copy, x_copy, z_copy, x_forward, z_forward):
            make(piece).wait_send()
        return 0

    lax.fori_loop(0, PIECES, drain, 0)


def on_device(spectra, pair_bins, dead_mask):
    e1, e2 = tables()
    dma = pltpu.SemaphoreType.DMA
    return pl.pallas_call(
        kernel,
        out_shape=jax.ShapeDtypeStruct((1, LAGS), F32),
        in_specs=[
            pl.BlockSpec(memory_space=pltpu.SMEM),
            pl.BlockSpec(memory_space=pl.ANY),
            pl.BlockSpec(memory_space=pltpu.VMEM),
            pl.BlockSpec(memory_space=pl.ANY),
            pl.BlockSpec(memory_space=pl.ANY),
        ],
        out_specs=pl.BlockSpec(memory_space=pltpu.VMEM),
        scratch_shapes=[
            pltpu.VMEM((CB, W, 2 * F), BF16),
            pltpu.VMEM((2, 2 * CHUNKS * CB, 128), F32),
            pltpu.VMEM((CHUNKS, CB, 256), BF16),
            pltpu.VMEM((ROUNDS, CHUNKS, CB, 256), BF16),
            pltpu.VMEM((CHUNKS, CB, 256), BF16),
            pltpu.VMEM((CB, 128), jnp.int32),
            pltpu.VMEM((ROUNDS, CB, 128), jnp.int32),
            pltpu.VMEM((2, NB, CB * 128), BF16),
            pltpu.VMEM((CB, HALF, 256), BF16),
            pltpu.VMEM((N_ROW, NB // N_ROW, F), BF16),
            pltpu.VMEM((N_ROW - 1, NB // N_ROW, F), BF16),
            pltpu.VMEM((N_COL * 8, 128), F32),
            pltpu.VMEM((N_COL - 1, 8, 128), F32),
            pltpu.VMEM(e1.shape, F32),
            pltpu.VMEM(e2.shape, BF16),
            dma((3,)), dma((ROUNDS,)), dma((ROUNDS,)),
            dma((3, PIECES)), dma((3, PIECES)), dma((2, PIECES)), dma((2, PIECES)),
            dma((N_ROW - 1,)), dma((N_ROW - 1,)), dma((N_COL - 1,)), dma((N_COL - 1,)),
        ],
        compiler_params=pltpu.CompilerParams(
            collective_id=0, has_side_effects=True, vmem_limit_bytes=48 << 20),
        name="correlate",
    )(dead_mask, spectra, pair_bins, jnp.asarray(e1), jnp.asarray(e2))


def solution(mesh):
    return jax.shard_map(
        on_device,
        mesh=mesh,
        in_specs=(P(("row", "col"), None, None), P(None, ("row", "col"), None), P(("row", "col"))),
        out_specs=P(("row", "col"), None),
        check_vma=False,
    )
```

```python
import functools
import math

import jax
import jax.numpy as jnp
import numpy as np
from jax import lax
from jax.experimental import pallas as pl
from jax.experimental.pallas import tpu as pltpu
from jax.sharding import PartitionSpec as P

NT = 1600
LAGS = 896
NB = 128
ROUNDS = 4
CB = 32
W = 8
F = 768
N_ROW = 8
N_COL = 16
FC = 16
HALF = F // 2
CHUNKS = HALF // FC
PIECES = 6
CP = CHUNKS // PIECES
LAG = 3
GROUPS = HALF // 128
MESH = pl.DeviceIdType.MESH
F32 = jnp.float32
BF16 = jnp.bfloat16


def tables():
    at = np.arange(F, dtype=np.int64)
    k = at // 128 * 128 + -(at % 128 // FC) % 8 * FC + at % FC
    scale = 1.0 / (2.0 * math.sqrt(F * W * (ROUNDS * CB * CB * N_ROW * N_COL // NB)))
    weight = np.where(k == 0, 1.0, 2.0) * scale
    start = 128 * np.arange(8, dtype=np.int64) - LAGS // 2
    first = (start[:, None] * k[None, :] % NT) * (2.0 * np.pi / NT)
    cos1 = (np.cos(first) * weight).reshape(8, 2, HALF).transpose(1, 0, 2)
    sin1 = (np.sin(first) * weight).reshape(8, 2, HALF).transpose(1, 0, 2)
    e1 = np.stack([cos1, sin1], axis=1).astype(np.float32)
    second = (k[:, None] * np.arange(128, dtype=np.int64)[None, :] % NT) * (2.0 * np.pi / NT)
    cos2 = np.cos(second).reshape(2, HALF, 128)
    sin2 = -np.sin(second).reshape(2, HALF, 128)
    e2 = np.concatenate([cos2, sin2], axis=1).astype(np.float32)
    high = e2.astype(jnp.bfloat16)
    low = (e2 - high.astype(np.float32)).astype(jnp.bfloat16)
    return e1, np.stack([high, low], axis=0)


def flip(value, mask):
    for bit in range(4):
        if mask >> bit & 1:
            value = value + (1 << bit) * (1 - 2 * ((value // (1 << bit)) % 2))
    return value


def nt_dot(a, b):
    return lax.dot_general(a, b, (((1,), (1,)), ((), ())), preferred_element_type=F32)


def kernel(
    alive_hbm, spec_hbm, bins_hbm, e1_hbm, e2_hbm, out_ref,
    alive_ref, bins_ref, scale_v, x_v, d_v, send_v, recv_v, pbs_v, pbr_v, oh_v, cross_v, part_v, rows_v, s2_v, r2_v, e1_v, e2_v,
    local_sem, pb_ss, pb_rs, a_ss, a_rs, f_ss, f_rs, row_ss, row_rs, col_ss, col_rs,
):
    row = lax.axis_index("row")
    col = lax.axis_index("col")
    parity = (col + col // 2 + col // 4 + col // 8) % 2

    def device(mask):
        return (flip(row, mask >> 4), flip(col, mask & 15))

    loads = [
        pltpu.make_async_copy(source, target, local_sem.at[n])
        for n, (source, target) in enumerate([
            (bins_hbm, bins_ref), (alive_hbm, alive_ref), (spec_hbm, x_v), (e1_hbm, e1_v), (e2_hbm, e2_v)])
    ]
    for load in loads:
        load.start()

    peers = sorted({16 * k for k in range(1, N_ROW)} | set(range(1, N_COL)))
    barrier = pltpu.get_barrier_semaphore()
    for mask in peers:
        pl.semaphore_signal(barrier, inc=1, device_id=device(mask), device_id_type=MESH)

    loads[0].wait()
    bins = bins_ref[...].reshape(ROUNDS * CB, CB)
    padded = jnp.concatenate([bins, jnp.zeros((128, 96), jnp.int32)], axis=1).astype(F32)
    pbs_v[...] = padded.T[:CB, :].astype(jnp.int32)
    loads[1].wait()
    loads[2].wait()

    def scales(i, _):
        x = x_v[i].astype(F32)
        power = jnp.mean(x * x, axis=-1, keepdims=True)
        alive = alive_ref[i].astype(F32)
        scale_v[i] = jnp.broadcast_to(alive / jnp.sqrt(power + 1e-06), (W, 128))
        return 0

    lax.fori_loop(0, CB, scales, 0, unroll=8)

    lane = lax.broadcasted_iota(jnp.int32, (8, 128), 1) // 16
    bits = [(lane // (1 << s)) % 2 == 1 for s in range(3)]

    def whiten(ft):
        def one(i, _):
            for c in range(2):
                at = pl.multiple_of(c * F + ft * 128, 128)
                t = x_v[i, :, pl.ds(at, 128)].astype(F32) * scale_v[i]
                t = pltpu.roll(t, 0, 1, stride=16, stride_axis=0)
                for s in range(3):
                    t = jnp.where(bits[s], pltpu.roll(t, 8 - (1 << s), 0), t)
                d_v[c, pl.ds(ft * 8 * CB + i, 8, stride=CB), :] = t
            return 0

        lax.fori_loop(0, CB, one, 0, unroll=8)

    def span(piece):
        return pl.ds(piece * CP, CP)

    def core_copy(piece):
        return pltpu.make_async_remote_copy(
            src_ref=send_v.at[span(piece)], dst_ref=recv_v.at[0, span(piece)],
            send_sem=a_ss.at[0, piece], recv_sem=a_rs.at[0, piece], device_id=device(1), device_id_type=MESH)

    def x_copy(piece):
        return pltpu.make_async_remote_copy(
            src_ref=send_v.at[span(piece)], dst_ref=recv_v.at[2, span(piece)],
            send_sem=a_ss.at[1, piece], recv_sem=a_rs.at[1, piece], device_id=device(4), device_id_type=MESH)

    def z_copy(piece):
        return pltpu.make_async_remote_copy(
            src_ref=send_v.at[span(piece)], dst_ref=recv_v.at[1, span(piece)],
            send_sem=a_ss.at[2, piece], recv_sem=a_rs.at[2, piece], device_id=device(2), device_id_type=MESH)

    def x_forward(piece):
        return pltpu.make_async_remote_copy(
            src_ref=recv_v.at[2, span(piece)], dst_ref=recv_v.at[3, span(piece)],
            send_sem=f_ss.at[piece], recv_sem=f_rs.at[piece], device_id=device(12), device_id_type=MESH)

    bin_copies = [
        pltpu.make_async_remote_copy(
            src_ref=pbs_v, dst_ref=pbr_v.at[r], send_sem=pb_ss.at[r], recv_sem=pb_rs.at[r],
            device_id=device(1 << r), device_id_type=MESH)
        for r in range(ROUNDS)
    ]

    def send(group, _):
        whiten((1 - parity) * GROUPS + group)

        def pack(k, _):
            q = group * 8 + k
            start = pl.multiple_of(((1 - parity) * CHUNKS + q) * CB, CB)
            for c in range(2):
                send_v[q, :, c * 128 : c * 128 + 128] = d_v[c, pl.ds(start, CB), :].astype(BF16)
            return 0

        lax.fori_loop(0, 8, pack, 0, unroll=2)

        @pl.when(group == 0)
        def _():
            pl.semaphore_wait(barrier, len(peers))
            for copy in bin_copies:
                copy.start()

        def start(piece, _):
            x_copy(piece).start()
            z_copy(piece).start()
            core_copy(piece).start()
            return 0

        lax.fori_loop(group * (8 // CP), (group + 1) * (8 // CP), start, 0)
        return 0

    lax.fori_loop(0, GROUPS, send, 0)

    def rest(group, _):
        whiten(parity * GROUPS + group)
        return 0

    lax.fori_loop(0, GROUPS, rest, 0)

    def forward(piece):
        x_copy(piece).wait_recv()
        x_forward(piece).start()

    forward(0)
    for copy in bin_copies:
        copy.wait()
    own = jnp.concatenate([bins_ref[r] for r in range(ROUNDS)], axis=1)
    of_round = lax.broadcasted_iota(jnp.int32, (CB, 128), 1) // CB
    other = pbr_v[0]
    for r in range(1, ROUNDS):
        other = jnp.where(of_round == r, pbr_v[r], other)
    bin_ids = lax.broadcasted_iota(jnp.int32, (NB, 128), 0)
    for i in range(CB):
        one = (own[i : i + 1, :] == bin_ids).astype(F32)
        two = (other[i : i + 1, :] == bin_ids).astype(F32)
        oh_v[0, :, i * 128 : i * 128 + 128] = (one + two).astype(BF16)
        oh_v[1, :, i * 128 : i * 128 + 128] = (one - two).astype(BF16)

    forward(1)
    forward(2)

    mask = (
        lax.broadcasted_iota(jnp.int32, (FC, 256), 1) % FC == lax.broadcasted_iota(jnp.int32, (FC, 256), 0)
    ).astype(F32).astype(BF16)

    def products(q, _):
        start = (parity * CHUNKS + q) * CB
        parts = []
        for i in range(CB):
            v = [d_v[c, pl.ds(start + i, 8, stride=0), :] for c in range(2)]
            v = jnp.concatenate([jnp.concatenate([u, u], axis=0).astype(BF16) for u in v], axis=1)
            parts.append(v * mask)
        lhs = jnp.concatenate(parts, axis=0)
        other_part = recv_v[:, q].reshape(ROUNDS * CB, 256)
        turned = jnp.concatenate([-other_part[:, 128:], other_part[:, :128]], axis=1)
        rhs = jnp.concatenate([other_part, turned], axis=0)
        cross = nt_dot(lhs, rhs).astype(BF16)
        cross_v[:, pl.ds(pl.multiple_of(q * FC, FC), FC), :] = cross.reshape(CB, FC, 256)
        return 0

    def row_copy(g, k):
        return pltpu.make_async_remote_copy(
            src_ref=part_v.at[g, flip(row, k)], dst_ref=rows_v.at[g, k - 1],
            send_sem=row_ss.at[g, k - 1], recv_sem=row_rs.at[g, k - 1],
            device_id=device(16 * k), device_id_type=MESH)

    def stack(g):
        for c in range(2):
            at = pl.ds(pl.multiple_of(g * 128, 128), 128)
            values = jnp.concatenate([cross_v[i, at, c * 128 : c * 128 + 128] for i in range(CB)], axis=1)
            total = nt_dot(oh_v[c], values)
            part_v[g, :, :, c * 128 : c * 128 + 128] = total.astype(BF16).reshape(N_ROW, NB // N_ROW, 128)
        for k in range(1, N_ROW):
            row_copy(g, k).start()

    def step(piece, _):
        @pl.when(piece < PIECES)
        def _():
            forward(piece)

        before = piece - LAG
        core_copy(before).wait_recv()
        z_copy(before).wait_recv()
        x_forward(before).wait_recv()
        lax.fori_loop(0, CP, lambda k, _: products(before * CP + k, _), 0, unroll=CP)

        @pl.when(before % 2 == 1)
        def _():
            stack(before // 2)
        return 0

    lax.fori_loop(LAG, PIECES + LAG, step, 0)

    for g in range(GROUPS):
        total = part_v[g, row].astype(F32)
        for k in range(1, N_ROW):
            row_copy(g, k).wait_recv()
            total = total + rows_v[g, k - 1].astype(F32)
        for c in range(2):
            s2_v[pl.ds(c * GROUPS + g, N_COL, stride=8), :] = total[:, c * 128 : c * 128 + 128]

    col_copies = [
        pltpu.make_async_remote_copy(
            src_ref=s2_v.at[pl.ds(pl.multiple_of(flip(col, k) * 8, 8), 8), :], dst_ref=r2_v.at[k - 1],
            send_sem=col_ss.at[k - 1], recv_sem=col_rs.at[k - 1], device_id=device(k), device_id_type=MESH)
        for k in range(1, N_COL)
    ]
    for copy in col_copies:
        copy.start()
    loads[3].wait()
    loads[4].wait()
    sums = [s2_v[pl.ds(pl.multiple_of(col * 8, 8), 8), :], None]
    for k, copy in enumerate(col_copies, 1):
        copy.wait_recv()
        odd = bin(k).count("1") % 2
        sums[odd] = r2_v[k - 1] if sums[odd] is None else sums[odd] + r2_v[k - 1]

    result = None
    for which in range(2):
        half = parity if which == 0 else 1 - parity
        x = sums[which]
        reals, imags = [], []
        for ft in range(3):
            cos1 = e1_v[half, 0, :, ft * 128 : ft * 128 + 128]
            sin1 = e1_v[half, 1, :, ft * 128 : ft * 128 + 128]
            re, im = x[ft : ft + 1, :], x[3 + ft : 4 + ft, :]
            reals.append(re * cos1 - im * sin1)
            imags.append(re * sin1 + im * cos1)
        turned = jnp.concatenate(reals + imags, axis=1)
        high = turned.astype(BF16)
        low = (turned - high.astype(F32)).astype(BF16)
        both = jnp.concatenate([high, low], axis=0)
        for part in range(2):
            o = jnp.dot(both, e2_v[part, half], preferred_element_type=F32)
            o = o[:8] + o[8:]
            result = o if result is None else result + o
    for mh in range(LAGS // 128):
        out_ref[0:1, mh * 128 : mh * 128 + 128] = result[mh : mh + 1, :]

    for copy in col_copies:
        copy.wait_send()
    for g in range(GROUPS):
        for k in range(1, N_ROW):
            row_copy(g, k).wait_send()

    def drain(piece, _):
        for make in (core_copy, x_copy, z_copy, x_forward):
            make(piece).wait_send()
        return 0

    lax.fori_loop(0, PIECES, drain, 0)


def on_device(spectra, pair_bins, dead_mask):
    e1, e2 = tables()
    dma = pltpu.SemaphoreType.DMA
    return pl.pallas_call(
        kernel,
        out_shape=jax.ShapeDtypeStruct((1, LAGS), F32),
        in_specs=[pl.BlockSpec(memory_space=pl.ANY)] * 5,
        out_specs=pl.BlockSpec(memory_space=pltpu.VMEM),
        scratch_shapes=[
            pltpu.SMEM((CB,), jnp.int32),
            pltpu.VMEM((ROUNDS, CB, CB), jnp.int32),
            pltpu.VMEM((CB, W, 128), F32),
            pltpu.VMEM((CB, W, 2 * F), BF16),
            pltpu.VMEM((2, 2 * CHUNKS * CB, 128), F32),
            pltpu.VMEM((CHUNKS, CB, 256), BF16),
            pltpu.VMEM((ROUNDS, CHUNKS, CB, 256), BF16),
            pltpu.VMEM((CB, 128), jnp.int32),
            pltpu.VMEM((ROUNDS, CB, 128), jnp.int32),
            pltpu.VMEM((2, NB, CB * 128), BF16),
            pltpu.VMEM((CB, HALF, 256), BF16),
            pltpu.VMEM((GROUPS, N_ROW, NB // N_ROW, 256), BF16),
            pltpu.VMEM((GROUPS, N_ROW - 1, NB // N_ROW, 256), BF16),
            pltpu.VMEM((N_COL * 8, 128), F32),
            pltpu.VMEM((N_COL - 1, 8, 128), F32),
            pltpu.VMEM(e1.shape, F32),
            pltpu.VMEM(e2.shape, BF16),
            dma((5,)), dma((ROUNDS,)), dma((ROUNDS,)),
            dma((3, PIECES)), dma((3, PIECES)), dma((PIECES,)), dma((PIECES,)),
            dma((GROUPS, N_ROW - 1)), dma((GROUPS, N_ROW - 1)), dma((N_COL - 1,)), dma((N_COL - 1,)),
        ],
        compiler_params=pltpu.CompilerParams(
            collective_id=0, has_side_effects=True, vmem_limit_bytes=64 << 20),
        name="correlate",
    )(dead_mask, spectra, pair_bins, jnp.asarray(e1), jnp.asarray(e2))


def solution(mesh):
    return jax.shard_map(
        on_device,
        mesh=mesh,
        in_specs=(P(("row", "col"), None, None), P(None, ("row", "col"), None), P(("row", "col"))),
        out_specs=P(("row", "col"), None),
        check_vma=False,
    )
```

```python
import functools
import math

import jax
import jax.numpy as jnp
import numpy as np
from jax import lax
from jax.experimental import pallas as pl
from jax.experimental.pallas import tpu as pltpu
from jax.sharding import PartitionSpec as P

NT = 1600
LAGS = 896
NB = 128
ROUNDS = 4
CB = 32
W = 8
F = 768
N_ROW = 8
N_COL = 16
FC = 16
HALF = F // 2
CHUNKS = HALF // FC
PIECES = 6
CP = CHUNKS // PIECES
LAG = 4
GROUPS = HALF // 128
NEAR = 8
FAR = 16
STACKS = ((0, 256), (256, 128))
MESH = pl.DeviceIdType.MESH
F32 = jnp.float32
BF16 = jnp.bfloat16


def tables():
    at = np.arange(F, dtype=np.int64)
    k = at // 128 * 128 + -(at % 128 // FC) % 8 * FC + at % FC
    scale = 1.0 / (2.0 * math.sqrt(F * W * (ROUNDS * CB * CB * N_ROW * N_COL // NB)))
    weight = np.where(k == 0, 1.0, 2.0) * scale
    start = 128 * np.arange(8, dtype=np.int64) - LAGS // 2
    first = (start[:, None] * k[None, :] % NT) * (2.0 * np.pi / NT)
    cos1 = (np.cos(first) * weight).reshape(8, 2, HALF).transpose(1, 0, 2)
    sin1 = (np.sin(first) * weight).reshape(8, 2, HALF).transpose(1, 0, 2)
    e1 = np.stack([cos1, sin1], axis=1).astype(np.float32)
    second = (k[:, None] * np.arange(128, dtype=np.int64)[None, :] % NT) * (2.0 * np.pi / NT)
    cos2 = np.cos(second).reshape(2, HALF, 128)
    sin2 = -np.sin(second).reshape(2, HALF, 128)
    e2 = np.concatenate([cos2, sin2], axis=1).astype(np.float32)
    high = e2.astype(jnp.bfloat16)
    low = (e2 - high.astype(np.float32)).astype(jnp.bfloat16)
    return e1, np.stack([high, low], axis=0)


def flip(value, mask):
    for bit in range(4):
        if mask >> bit & 1:
            value = value + (1 << bit) * (1 - 2 * ((value // (1 << bit)) % 2))
    return value


def links(mask):
    steps = (0, 1, 2, 1)
    x, y, z = mask >> 2 & 3, mask >> 5 & 3, (mask >> 4 & 1) + (mask & 2)
    return steps[x] + steps[y] + steps[z]


def nt_dot(a, b):
    return lax.dot_general(a, b, (((1,), (1,)), ((), ())), preferred_element_type=F32)


def kernel(
    alive_hbm, spec_hbm, bins_hbm, e1_hbm, e2_hbm, out_ref,
    alive_ref, bins_ref, scale_v, x_v, d_v, send_v, recv_v, pbs_v, pbr_v, oh_v, cross_v, part0_v, part1_v, near0_v, near1_v, s2_v, r2_v, e1_v, e2_v,
    local_sem, pb_ss, pb_rs, a_ss, a_rs, f_ss, f_rs, near_ss, near_rs, far_ss, far_rs, entered,
):
    parts, nears = (part0_v, part1_v), (near0_v, near1_v)
    row = lax.axis_index("row")
    col = lax.axis_index("col")
    near = col // 4 * 2 + col % 2
    far = row * 2 + col // 2 % 2
    parity = (col + col // 2 + col // 4 + col // 8) % 2

    def device(mask):
        return (flip(row, mask >> 4), flip(col, mask & 15))

    loads = [
        pltpu.make_async_copy(source, target, local_sem.at[n])
        for n, (source, target) in enumerate([
            (bins_hbm, bins_ref), (alive_hbm, alive_ref), (spec_hbm, x_v), (e1_hbm, e1_v), (e2_hbm, e2_v)])
    ]
    for load in loads:
        load.start()

    peers = sorted([1, 4, 5, 8, 9, 12, 13, 2, 16, 18, 32, 64, 96], key=links, reverse=True)
    barrier = pltpu.get_barrier_semaphore()
    for mask in peers:
        pl.semaphore_signal(barrier, inc=1, device_id=device(mask), device_id_type=MESH)

    loads[0].wait()
    bins = bins_ref[...].reshape(ROUNDS * CB, CB)
    padded = jnp.concatenate([bins, jnp.zeros((128, 96), jnp.int32)], axis=1).astype(F32)
    pbs_v[...] = padded.T[:CB, :].astype(jnp.int32)
    loads[1].wait()
    loads[2].wait()

    def scales(i, _):
        x = x_v[i].astype(F32)
        power = jnp.mean(x * x, axis=-1, keepdims=True)
        alive = alive_ref[i].astype(F32)
        scale_v[i] = jnp.broadcast_to(alive / jnp.sqrt(power + 1e-06), (W, 128))
        return 0

    lax.fori_loop(0, CB, scales, 0, unroll=8)

    lane = lax.broadcasted_iota(jnp.int32, (8, 128), 1) // 16
    bits = [(lane // (1 << s)) % 2 == 1 for s in range(3)]

    def whiten(ft):
        def one(i, _):
            for c in range(2):
                at = pl.multiple_of(c * F + ft * 128, 128)
                t = x_v[i, :, pl.ds(at, 128)].astype(F32) * scale_v[i]
                t = pltpu.roll(t, 0, 1, stride=16, stride_axis=0)
                for s in range(3):
                    t = jnp.where(bits[s], pltpu.roll(t, 8 - (1 << s), 0), t)
                d_v[c, pl.ds(ft * 8 * CB + i, 8, stride=CB), :] = t
            return 0

        lax.fori_loop(0, CB, one, 0, unroll=8)

    def span(piece):
        return pl.ds(piece * CP, CP)

    def core_copy(piece):
        return pltpu.make_async_remote_copy(
            src_ref=send_v.at[span(piece)], dst_ref=recv_v.at[0, span(piece)],
            send_sem=a_ss.at[0, piece], recv_sem=a_rs.at[0, piece], device_id=device(1), device_id_type=MESH)

    def x_copy(piece):
        return pltpu.make_async_remote_copy(
            src_ref=send_v.at[span(piece)], dst_ref=recv_v.at[2, span(piece)],
            send_sem=a_ss.at[1, piece], recv_sem=a_rs.at[1, piece], device_id=device(4), device_id_type=MESH)

    def z_copy(piece):
        return pltpu.make_async_remote_copy(
            src_ref=send_v.at[span(piece)], dst_ref=recv_v.at[1, span(piece)],
            send_sem=a_ss.at[2, piece], recv_sem=a_rs.at[2, piece], device_id=device(2), device_id_type=MESH)

    def x_forward(piece):
        return pltpu.make_async_remote_copy(
            src_ref=recv_v.at[2, span(piece)], dst_ref=recv_v.at[3, span(piece)],
            send_sem=f_ss.at[piece], recv_sem=f_rs.at[piece], device_id=device(12), device_id_type=MESH)

    bin_copies = [
        pltpu.make_async_remote_copy(
            src_ref=pbs_v, dst_ref=pbr_v.at[r], send_sem=pb_ss.at[r], recv_sem=pb_rs.at[r],
            device_id=device(1 << r), device_id_type=MESH)
        for r in range(ROUNDS)
    ]

    def send(group, _):
        whiten((1 - parity) * GROUPS + group)

        def pack(k, _):
            q = group * 8 + k
            start = pl.multiple_of(((1 - parity) * CHUNKS + q) * CB, CB)
            for c in range(2):
                send_v[q, :, c * 128 : c * 128 + 128] = d_v[c, pl.ds(start, CB), :].astype(BF16)
            return 0

        lax.fori_loop(0, 8, pack, 0, unroll=2)

        @pl.when(group == 0)
        def _():
            pl.semaphore_wait(barrier, len(peers))
            for copy in bin_copies:
                copy.start()

        pieces = [group * (8 // CP) + k for k in range(8 // CP)]
        for piece in pieces:
            for make in (x_copy, z_copy, core_copy):
                make(piece).start()

        @pl.when(group == 0)
        def _():
            for along_z in (2, 16, 18):
                pl.semaphore_signal(entered, inc=1, device_id=device(along_z), device_id_type=MESH)
        return 0

    lax.fori_loop(0, GROUPS, send, 0)

    def rest(group, _):
        whiten(parity * GROUPS + group)
        return 0

    lax.fori_loop(0, GROUPS, rest, 0)

    def forward(piece):
        x_copy(piece).wait_recv()
        x_forward(piece).start()

    forward(0)
    forward(1)
    for copy in bin_copies:
        copy.wait()
    own = jnp.concatenate([bins_ref[r] for r in range(ROUNDS)], axis=1)
    of_round = lax.broadcasted_iota(jnp.int32, (CB, 128), 1) // CB
    other = pbr_v[0]
    for r in range(1, ROUNDS):
        other = jnp.where(of_round == r, pbr_v[r], other)
    place = lax.broadcasted_iota(jnp.int32, (NB, 128), 0)
    bin_ids = place // 2 % 8 * 16 + place // 32 * 4 + place % 2 * 2 + place // 16 % 2
    for i in range(CB):
        one = (own[i : i + 1, :] == bin_ids).astype(F32)
        two = (other[i : i + 1, :] == bin_ids).astype(F32)
        oh_v[0, :, i * 128 : i * 128 + 128] = (one + two).astype(BF16)
        oh_v[1, :, i * 128 : i * 128 + 128] = (one - two).astype(BF16)

    for k in range(2, LAG):
        forward(k)

    mask = (
        lax.broadcasted_iota(jnp.int32, (FC, 256), 1) % FC == lax.broadcasted_iota(jnp.int32, (FC, 256), 0)
    ).astype(F32).astype(BF16)

    def products(q, _):
        start = (parity * CHUNKS + q) * CB
        parts = []
        for i in range(CB):
            v = [d_v[c, pl.ds(start + i, 8, stride=0), :] for c in range(2)]
            v = jnp.concatenate([jnp.concatenate([u, u], axis=0).astype(BF16) for u in v], axis=1)
            parts.append(v * mask)
        lhs = jnp.concatenate(parts, axis=0)
        other_part = recv_v[:, q].reshape(ROUNDS * CB, 256)
        turned = jnp.concatenate([-other_part[:, 128:], other_part[:, :128]], axis=1)
        rhs = jnp.concatenate([other_part, turned], axis=0)
        cross = nt_dot(lhs, rhs).astype(BF16)
        cross_v[:, pl.ds(pl.multiple_of(q * FC, FC), FC), :] = cross.reshape(CB, FC, 256)
        return 0

    near_mask = [k // 2 * 4 + k % 2 for k in range(NEAR)]
    far_mask = [k // 2 * 16 + k % 2 * 2 for k in range(FAR)]
    near_order = sorted(range(1, NEAR), key=lambda k: -links(near_mask[k]))
    far_order = sorted(range(1, FAR), key=lambda k: -links(far_mask[k]))

    def near_copy(g, k):
        return pltpu.make_async_remote_copy(
            src_ref=parts[g].at[flip(near, k)], dst_ref=nears[g].at[k - 1],
            send_sem=near_ss.at[g, k - 1], recv_sem=near_rs.at[g, k - 1],
            device_id=device(near_mask[k]), device_id_type=MESH)

    def stack(g):
        first, count = STACKS[g]
        for c in range(2):
            values = jnp.concatenate(
                [cross_v[i, first : first + count, c * 128 : c * 128 + 128] for i in range(CB)], axis=1)
            total = nt_dot(oh_v[c], values)
            parts[g][:, :, c * count : c * count + count] = total.astype(BF16).reshape(NEAR, FAR, count)
        for k in near_order:
            near_copy(g, k).start()

    def step(piece, _):
        @pl.when(piece < PIECES)
        def _():
            forward(piece)

        before = piece - LAG
        core_copy(before).wait_recv()
        z_copy(before).wait_recv()
        x_forward(before).wait_recv()
        lax.fori_loop(0, CP, lambda k, _: products(before * CP + k, _), 0, unroll=CP)

        for g, (first, count) in enumerate(STACKS):
            @pl.when(before == (first + count) // (FC * CP) - 1)
            def _():
                stack(g)
        return 0

    lax.fori_loop(LAG, PIECES + LAG, step, 0)

    def drain(piece, _):
        for make in (core_copy, x_copy, z_copy, x_forward):
            make(piece).wait_send()
        return 0

    lax.fori_loop(0, PIECES, drain, 0)

    for g, (first, count) in enumerate(STACKS):
        totals = [parts[g][near].astype(F32), None]
        for k in range(1, NEAR):
            near_copy(g, k).wait_recv()
            value = nears[g][k - 1].astype(F32)
            odd = bin(near_mask[k]).count("1") % 2
            totals[odd] = value if totals[odd] is None else totals[odd] + value
        for odd in range(2):
            half = parity if odd == 0 else 1 - parity
            for c in range(2):
                for n in range(count // 128):
                    at = half * 8 + c * GROUPS + first // 128 + n
                    value = totals[odd][:, c * count + n * 128 : c * count + n * 128 + 128]
                    s2_v[pl.ds(at, FAR, stride=16), :] = value

    far_copies = [
        pltpu.make_async_remote_copy(
            src_ref=s2_v.at[pl.ds(pl.multiple_of(flip(far, k) * 16, 16), 16), :], dst_ref=r2_v.at[k - 1],
            send_sem=far_ss.at[k - 1], recv_sem=far_rs.at[k - 1],
            device_id=device(far_mask[k]), device_id_type=MESH)
        for k in far_order
    ]
    pl.semaphore_wait(entered, 3)
    for copy in far_copies:
        copy.start()
    for g in range(len(STACKS)):
        for k in range(1, NEAR):
            near_copy(g, k).wait_send()
    loads[3].wait()
    loads[4].wait()
    sums = s2_v[pl.ds(pl.multiple_of(far * 16, 16), 16), :]
    for k, copy in zip(far_order, far_copies):
        copy.wait_recv()
        sums = sums + r2_v[k - 1]

    result = None
    for half in range(2):
        x = sums[half * 8 : half * 8 + 8]
        reals, imags = [], []
        for ft in range(3):
            cos1 = e1_v[half, 0, :, ft * 128 : ft * 128 + 128]
            sin1 = e1_v[half, 1, :, ft * 128 : ft * 128 + 128]
            re, im = x[ft : ft + 1, :], x[3 + ft : 4 + ft, :]
            reals.append(re * cos1 - im * sin1)
            imags.append(re * sin1 + im * cos1)
        turned = jnp.concatenate(reals + imags, axis=1)
        high = turned.astype(BF16)
        low = (turned - high.astype(F32)).astype(BF16)
        both = jnp.concatenate([high, low], axis=0)
        for part in range(2):
            o = jnp.dot(both, e2_v[part, half], preferred_element_type=F32)
            o = o[:8] + o[8:]
            result = o if result is None else result + o
    for mh in range(LAGS // 128):
        out_ref[0:1, mh * 128 : mh * 128 + 128] = result[mh : mh + 1, :]

    for copy in far_copies:
        copy.wait_send()


def on_device(spectra, pair_bins, dead_mask):
    e1, e2 = tables()
    dma = pltpu.SemaphoreType.DMA
    return pl.pallas_call(
        kernel,
        out_shape=jax.ShapeDtypeStruct((1, LAGS), F32),
        in_specs=[pl.BlockSpec(memory_space=pl.ANY)] * 5,
        out_specs=pl.BlockSpec(memory_space=pltpu.VMEM),
        scratch_shapes=[
            pltpu.SMEM((CB,), jnp.int32),
            pltpu.VMEM((ROUNDS, CB, CB), jnp.int32),
            pltpu.VMEM((CB, W, 128), F32),
            pltpu.VMEM((CB, W, 2 * F), BF16),
            pltpu.VMEM((2, 2 * CHUNKS * CB, 128), F32),
            pltpu.VMEM((CHUNKS, CB, 256), BF16),
            pltpu.VMEM((ROUNDS, CHUNKS, CB, 256), BF16),
            pltpu.VMEM((CB, 128), jnp.int32),
            pltpu.VMEM((ROUNDS, CB, 128), jnp.int32),
            pltpu.VMEM((2, NB, CB * 128), BF16),
            pltpu.VMEM((CB, HALF, 256), BF16),
            *[pltpu.VMEM((NEAR, FAR, 2 * count), BF16) for _, count in STACKS],
            *[pltpu.VMEM((NEAR - 1, FAR, 2 * count), BF16) for _, count in STACKS],
            pltpu.VMEM((FAR * 16, 128), F32),
            pltpu.VMEM((FAR - 1, 16, 128), F32),
            pltpu.VMEM(e1.shape, F32),
            pltpu.VMEM(e2.shape, BF16),
            dma((5,)), dma((ROUNDS,)), dma((ROUNDS,)),
            dma((3, PIECES)), dma((3, PIECES)), dma((PIECES,)), dma((PIECES,)),
            dma((len(STACKS), NEAR - 1)), dma((len(STACKS), NEAR - 1)), dma((FAR - 1,)), dma((FAR - 1,)),
            pltpu.SemaphoreType.REGULAR,
        ],
        compiler_params=pltpu.CompilerParams(
            collective_id=0, has_side_effects=True, vmem_limit_bytes=48 << 20),
        name="correlate",
    )(*[
        pltpu.with_memory_space_constraint(x, pltpu.HBM)
        for x in (dead_mask, spectra, pair_bins, jnp.asarray(e1), jnp.asarray(e2))
    ])


def solution(mesh):
    return jax.shard_map(
        on_device,
        mesh=mesh,
        in_specs=(P(("row", "col"), None, None), P(None, ("row", "col"), None), P(("row", "col"))),
        out_specs=P(("row", "col"), None),
        check_vma=False,
    )
```

```python
import functools
import math

import jax
import jax.numpy as jnp
import numpy as np
from jax import lax
from jax.experimental import pallas as pl
from jax.experimental.pallas import tpu as pltpu
from jax.sharding import PartitionSpec as P

NT = 1600
LAGS = 896
NB = 128
ROUNDS = 4
CB = 32
W = 8
F = 768
N_ROW = 8
N_COL = 16
FC = 16
HALF = F // 2
CHUNKS = HALF // FC
SPANS = ((0, 4), (4, 4), (8, 4), (12, 4), (16, 4), (20, 2), (22, 2))
PIECES = len(SPANS)
LAG = 4
GROUPS = HALF // 128
NEAR = 8
FAR = 16
STACKS = ((0, 256), (256, 128))
MESH = pl.DeviceIdType.MESH
F32 = jnp.float32
BF16 = jnp.bfloat16


def tables():
    at = np.arange(F, dtype=np.int64)
    k = at // 128 * 128 + -(at % 128 // FC) % 8 * FC + at % FC
    scale = 1.0 / (2.0 * math.sqrt(F * W * (ROUNDS * CB * CB * N_ROW * N_COL // NB)))
    weight = np.where(k == 0, 1.0, 2.0) * scale
    start = 128 * np.arange(8, dtype=np.int64) - LAGS // 2
    first = (start[:, None] * k[None, :] % NT) * (2.0 * np.pi / NT)
    cos1 = (np.cos(first) * weight).reshape(8, 2, HALF).transpose(1, 0, 2)
    sin1 = (np.sin(first) * weight).reshape(8, 2, HALF).transpose(1, 0, 2)
    e1 = np.stack([cos1, sin1], axis=1).astype(np.float32)
    second = (k[:, None] * np.arange(128, dtype=np.int64)[None, :] % NT) * (2.0 * np.pi / NT)
    cos2 = np.cos(second).reshape(2, HALF, 128)
    sin2 = -np.sin(second).reshape(2, HALF, 128)
    e2 = np.concatenate([cos2, sin2], axis=1).astype(np.float32)
    high = e2.astype(jnp.bfloat16)
    low = (e2 - high.astype(np.float32)).astype(jnp.bfloat16)
    return e1, np.stack([high, low], axis=0)


def flipper(value, bits):
    steps = [(1 << bit) * (1 - 2 * ((value // (1 << bit)) % 2)) for bit in range(bits)]

    def flip(mask):
        result = value
        for bit in range(bits):
            if mask >> bit & 1:
                result = result + steps[bit]
        return result

    return flip


def links(mask):
    steps = (0, 1, 2, 1)
    x, y, z = mask >> 2 & 3, mask >> 5 & 3, (mask >> 4 & 1) + (mask & 2)
    return steps[x] + steps[y] + steps[z]


def nt_dot(a, b):
    return lax.dot_general(a, b, (((1,), (1,)), ((), ())), preferred_element_type=F32)


def kernel(
    alive_hbm, spec_hbm, bins_hbm, e1_hbm, e2_hbm, out_ref,
    alive_ref, bins_ref, scale_v, x_v, d_v, send_v, recv_v, lhs_v, pbs_v, pbr_v, oh_v, cross_v, part0_v, part1_v, near0_v, near1_v, s2_v, r2_v, e1_v, e2_v,
    local_sem, pb_ss, pb_rs, a_ss, a_rs, f_ss, f_rs, near_ss, near_rs, far_ss, far_rs, entered,
):
    parts, nears = (part0_v, part1_v), (near0_v, near1_v)
    row = lax.axis_index("row")
    col = lax.axis_index("col")
    near = col // 4 * 2 + col % 2
    far = row * 2 + col // 2 % 2
    parity = (col + col // 2 + col // 4 + col // 8) % 2

    flip_row, flip_col, flip_near, flip_far = (
        flipper(value, bits) for value, bits in ((row, 3), (col, 4), (near, 3), (far, 4)))

    def device(mask):
        return (flip_row(mask >> 4), flip_col(mask & 15))

    loads = [
        pltpu.make_async_copy(source, target, local_sem.at[n])
        for n, (source, target) in enumerate([
            (bins_hbm, bins_ref), (alive_hbm, alive_ref), (spec_hbm, x_v), (e1_hbm, e1_v), (e2_hbm, e2_v)])
    ]
    for load in loads:
        load.start()

    peers = sorted([1, 4, 5, 8, 9, 12, 13, 2, 16, 18, 32, 64, 96], key=links, reverse=True)
    barrier = pltpu.get_barrier_semaphore()
    for mask in peers:
        pl.semaphore_signal(barrier, inc=1, device_id=device(mask), device_id_type=MESH)

    loads[0].wait()
    bins = bins_ref[...].reshape(ROUNDS * CB, CB)
    padded = jnp.concatenate([bins, jnp.zeros((128, 96), jnp.int32)], axis=1).astype(F32)
    pbs_v[...] = padded.T[:CB, :].astype(jnp.int32)
    loads[1].wait()
    loads[2].wait()

    def scales(i, _):
        x = x_v[i].astype(F32)
        power = jnp.mean(x * x, axis=-1, keepdims=True)
        alive = alive_ref[i].astype(F32)
        scale_v[i] = jnp.broadcast_to(alive / jnp.sqrt(power + 1e-06), (W, 128))
        return 0

    lax.fori_loop(0, CB, scales, 0, unroll=8)

    lane = lax.broadcasted_iota(jnp.int32, (8, 128), 1) // 16
    bits = [(lane // (1 << s)) % 2 == 1 for s in range(3)]

    def whiten(ft):
        def one(i, _):
            for c in range(2):
                at = pl.multiple_of(c * F + ft * 128, 128)
                t = x_v[i, :, pl.ds(at, 128)].astype(F32) * scale_v[i]
                t = pltpu.roll(t, 0, 1, stride=16, stride_axis=0)
                for s in range(3):
                    t = jnp.where(bits[s], pltpu.roll(t, 8 - (1 << s), 0), t)
                d_v[c, pl.ds(ft * 8 * CB + i, 8, stride=CB), :] = t
            return 0

        lax.fori_loop(0, CB, one, 0, unroll=8)

    def span(piece):
        return pl.ds(*SPANS[piece])

    def core_copy(piece):
        return pltpu.make_async_remote_copy(
            src_ref=send_v.at[span(piece)], dst_ref=recv_v.at[0, span(piece)],
            send_sem=a_ss.at[0, piece], recv_sem=a_rs.at[0, piece], device_id=device(1), device_id_type=MESH)

    def x_copy(piece):
        return pltpu.make_async_remote_copy(
            src_ref=send_v.at[span(piece)], dst_ref=recv_v.at[2, span(piece)],
            send_sem=a_ss.at[1, piece], recv_sem=a_rs.at[1, piece], device_id=device(4), device_id_type=MESH)

    def z_copy(piece):
        return pltpu.make_async_remote_copy(
            src_ref=send_v.at[span(piece)], dst_ref=recv_v.at[1, span(piece)],
            send_sem=a_ss.at[2, piece], recv_sem=a_rs.at[2, piece], device_id=device(2), device_id_type=MESH)

    def x_forward(piece):
        return pltpu.make_async_remote_copy(
            src_ref=recv_v.at[2, span(piece)], dst_ref=recv_v.at[3, span(piece)],
            send_sem=f_ss.at[piece], recv_sem=f_rs.at[piece], device_id=device(12), device_id_type=MESH)

    bin_copies = [
        pltpu.make_async_remote_copy(
            src_ref=pbs_v, dst_ref=pbr_v.at[r], send_sem=pb_ss.at[r], recv_sem=pb_rs.at[r],
            device_id=device(1 << r), device_id_type=MESH)
        for r in range(ROUNDS)
    ]

    def send(group, _):
        whiten((1 - parity) * GROUPS + group)

        def pack(k, _):
            q = group * 8 + k
            start = pl.multiple_of(((1 - parity) * CHUNKS + q) * CB, CB)
            for c in range(2):
                send_v[q, :, c * 128 : c * 128 + 128] = d_v[c, pl.ds(start, CB), :].astype(BF16)
            return 0

        lax.fori_loop(0, 8, pack, 0, unroll=2)

        if group == 0:
            pl.semaphore_wait(barrier, len(peers))
            for copy in bin_copies:
                copy.start()

        pieces = [k for k, (first, _) in enumerate(SPANS) if first // 8 == group]
        for piece in pieces:
            for make in (x_copy, z_copy, core_copy):
                make(piece).start()

        if group == 0:
            for along_z in (2, 16, 18):
                pl.semaphore_signal(entered, inc=1, device_id=device(along_z), device_id_type=MESH)
        return 0

    for group in range(GROUPS):
        send(group, 0)

    mask = (
        lax.broadcasted_iota(jnp.int32, (FC, 256), 1) % FC == lax.broadcasted_iota(jnp.int32, (FC, 256), 0)
    ).astype(F32).astype(BF16)

    def spread(q):
        start = (parity * CHUNKS + q) * CB
        for i in range(CB):
            v = [d_v[c, pl.ds(start + i, 8, stride=0), :] for c in range(2)]
            v = jnp.concatenate([jnp.concatenate([u, u], axis=0).astype(BF16) for u in v], axis=1)
            lhs_v[q, i * FC : i * FC + FC, :] = v * mask

    def rest(group, _):
        whiten(parity * GROUPS + group)

        def one(k, _):
            spread(group * 8 + k)
            return 0

        lax.fori_loop(0, 8, one, 0, unroll=2)
        return 0

    lax.fori_loop(0, GROUPS, rest, 0)

    def forward(piece):
        x_copy(piece).wait_recv()
        x_forward(piece).start()

    forward(0)
    forward(1)
    for copy in bin_copies:
        copy.wait()
    own = jnp.concatenate([bins_ref[r] for r in range(ROUNDS)], axis=1)
    of_round = lax.broadcasted_iota(jnp.int32, (CB, 128), 1) // CB
    other = pbr_v[0]
    for r in range(1, ROUNDS):
        other = jnp.where(of_round == r, pbr_v[r], other)
    place = lax.broadcasted_iota(jnp.int32, (NB, 128), 0)
    bin_ids = place // 2 % 8 * 16 + place // 32 * 4 + place % 2 * 2 + place // 16 % 2
    for i in range(CB):
        one = (own[i : i + 1, :] == bin_ids).astype(F32)
        two = (other[i : i + 1, :] == bin_ids).astype(F32)
        oh_v[0, :, i * 128 : i * 128 + 128] = (one + two).astype(BF16)
        oh_v[1, :, i * 128 : i * 128 + 128] = (one - two).astype(BF16)

    for k in range(2, LAG):
        forward(k)

    def products(q, _):
        other_part = recv_v[:, q].reshape(ROUNDS * CB, 256)
        turned = jnp.concatenate([-other_part[:, 128:], other_part[:, :128]], axis=1)
        rhs = jnp.concatenate([other_part, turned], axis=0)
        cross = nt_dot(lhs_v[q], rhs).astype(BF16)
        cross_v[:, pl.ds(pl.multiple_of(q * FC, FC), FC), :] = cross.reshape(CB, FC, 256)
        return 0

    near_mask = [k // 2 * 4 + k % 2 for k in range(NEAR)]
    far_mask = [k // 2 * 16 + k % 2 * 2 for k in range(FAR)]
    near_order = sorted(range(1, NEAR), key=lambda k: -links(near_mask[k]))
    far_order = sorted(range(1, FAR), key=lambda k: -links(far_mask[k]))

    def near_copy(g, k):
        return pltpu.make_async_remote_copy(
            src_ref=parts[g].at[flip_near(k)], dst_ref=nears[g].at[k - 1],
            send_sem=near_ss.at[g, k - 1], recv_sem=near_rs.at[g, k - 1],
            device_id=device(near_mask[k]), device_id_type=MESH)

    def stack(g):
        first, count = STACKS[g]
        for c in range(2):
            values = jnp.concatenate(
                [cross_v[i, first : first + count, c * 128 : c * 128 + 128] for i in range(CB)], axis=1)
            total = nt_dot(values, oh_v[c]).T
            parts[g][:, :, c * count : c * count + count] = total.astype(BF16).reshape(NEAR, FAR, count)
        for k in near_order:
            near_copy(g, k).start()

    for piece in range(LAG, PIECES + LAG):
        if piece < PIECES:
            forward(piece)
        before = piece - LAG
        core_copy(before).wait_recv()
        z_copy(before).wait_recv()
        x_forward(before).wait_recv()
        begin, number = SPANS[before]
        lax.fori_loop(0, number, lambda k, _: products(begin + k, _), 0, unroll=number)
        for g, (first, count) in enumerate(STACKS):
            if (begin + number) * FC == first + count:
                stack(g)

    def drain(piece, _):
        for make in (core_copy, x_copy, z_copy, x_forward):
            make(piece).wait_send()
        return 0

    for piece in range(PIECES):
        drain(piece, 0)

    for g, (first, count) in enumerate(STACKS):
        totals = [parts[g][near].astype(F32), None]
        for k in range(1, NEAR):
            near_copy(g, k).wait_recv()
            value = nears[g][k - 1].astype(F32)
            odd = bin(near_mask[k]).count("1") % 2
            totals[odd] = value if totals[odd] is None else totals[odd] + value
        for odd in range(2):
            half = parity if odd == 0 else 1 - parity
            for c in range(2):
                for n in range(count // 128):
                    at = half * 8 + c * GROUPS + first // 128 + n
                    value = totals[odd][:, c * count + n * 128 : c * count + n * 128 + 128]
                    s2_v[pl.ds(at, FAR, stride=16), :] = value

    far_copies = [
        pltpu.make_async_remote_copy(
            src_ref=s2_v.at[pl.ds(pl.multiple_of(flip_far(k) * 16, 16), 16), :], dst_ref=r2_v.at[k - 1],
            send_sem=far_ss.at[k - 1], recv_sem=far_rs.at[k - 1],
            device_id=device(far_mask[k]), device_id_type=MESH)
        for k in far_order
    ]
    pl.semaphore_wait(entered, 3)
    for copy in far_copies:
        copy.start()
    for g in range(len(STACKS)):
        for k in range(1, NEAR):
            near_copy(g, k).wait_send()
    loads[3].wait()
    loads[4].wait()
    sums = s2_v[pl.ds(pl.multiple_of(far * 16, 16), 16), :]
    for k, copy in zip(far_order, far_copies):
        copy.wait_recv()
        sums = sums + r2_v[k - 1]

    result = None
    for half in range(2):
        x = sums[half * 8 : half * 8 + 8]
        reals, imags = [], []
        for ft in range(3):
            cos1 = e1_v[half, 0, :, ft * 128 : ft * 128 + 128]
            sin1 = e1_v[half, 1, :, ft * 128 : ft * 128 + 128]
            re, im = x[ft : ft + 1, :], x[3 + ft : 4 + ft, :]
            reals.append(re * cos1 - im * sin1)
            imags.append(re * sin1 + im * cos1)
        turned = jnp.concatenate(reals + imags, axis=1)
        high = turned.astype(BF16)
        low = (turned - high.astype(F32)).astype(BF16)
        both = jnp.concatenate([high, low], axis=0)
        for part in range(2):
            o = jnp.dot(both, e2_v[part, half], preferred_element_type=F32)
            o = o[:8] + o[8:]
            result = o if result is None else result + o
    for mh in range(LAGS // 128):
        out_ref[0:1, mh * 128 : mh * 128 + 128] = result[mh : mh + 1, :]

    for copy in far_copies:
        copy.wait_send()


def on_device(spectra, pair_bins, dead_mask):
    e1, e2 = tables()
    dma = pltpu.SemaphoreType.DMA
    return pl.pallas_call(
        kernel,
        out_shape=jax.ShapeDtypeStruct((1, LAGS), F32),
        in_specs=[pl.BlockSpec(memory_space=pl.ANY)] * 5,
        out_specs=pl.BlockSpec(memory_space=pltpu.VMEM),
        scratch_shapes=[
            pltpu.SMEM((CB,), jnp.int32),
            pltpu.VMEM((ROUNDS, CB, CB), jnp.int32),
            pltpu.VMEM((CB, W, 128), F32),
            pltpu.VMEM((CB, W, 2 * F), BF16),
            pltpu.VMEM((2, 2 * CHUNKS * CB, 128), F32),
            pltpu.VMEM((CHUNKS, CB, 256), BF16),
            pltpu.VMEM((ROUNDS, CHUNKS, CB, 256), BF16),
            pltpu.VMEM((CHUNKS, CB * FC, 256), BF16),
            pltpu.VMEM((CB, 128), jnp.int32),
            pltpu.VMEM((ROUNDS, CB, 128), jnp.int32),
            pltpu.VMEM((2, NB, CB * 128), BF16),
            pltpu.VMEM((CB, HALF, 256), BF16),
            *[pltpu.VMEM((NEAR, FAR, 2 * count), BF16) for _, count in STACKS],
            *[pltpu.VMEM((NEAR - 1, FAR, 2 * count), BF16) for _, count in STACKS],
            pltpu.VMEM((FAR * 16, 128), F32),
            pltpu.VMEM((FAR - 1, 16, 128), F32),
            pltpu.VMEM(e1.shape, F32),
            pltpu.VMEM(e2.shape, BF16),
            dma((5,)), dma((ROUNDS,)), dma((ROUNDS,)),
            dma((3, PIECES)), dma((3, PIECES)), dma((PIECES,)), dma((PIECES,)),
            dma((len(STACKS), NEAR - 1)), dma((len(STACKS), NEAR - 1)), dma((FAR - 1,)), dma((FAR - 1,)),
            pltpu.SemaphoreType.REGULAR,
        ],
        compiler_params=pltpu.CompilerParams(
            collective_id=0, has_side_effects=True, vmem_limit_bytes=48 << 20),
        name="correlate",
    )(*[
        pltpu.with_memory_space_constraint(x, pltpu.HBM)
        for x in (dead_mask, spectra, pair_bins, jnp.asarray(e1), jnp.asarray(e2))
    ])


def solution(mesh):
    return jax.shard_map(
        on_device,
        mesh=mesh,
        in_specs=(P(("row", "col"), None, None), P(None, ("row", "col"), None), P(("row", "col"))),
        out_specs=P(("row", "col"), None),
        check_vma=False,
    )
```

```python
import functools
import math

import jax
import jax.numpy as jnp
import numpy as np
from jax import lax
from jax.experimental import pallas as pl
from jax.experimental.pallas import tpu as pltpu
from jax.sharding import PartitionSpec as P

NT = 1600
LAGS = 896
NB = 128
ROUNDS = 4
CB = 32
W = 8
F = 768
N_ROW = 8
N_COL = 16
FC = 16
HALF = F // 2
CHUNKS = HALF // FC
SPANS = ((0, 4), (4, 4), (8, 4), (12, 4), (16, 4), (20, 2), (22, 2))
PIECES = len(SPANS)
LAG = 4
GROUPS = HALF // 128
NEAR = 8
FAR = 16
STACKS = ((0, 256), (256, 128))
MESH = pl.DeviceIdType.MESH
F32 = jnp.float32
BF16 = jnp.bfloat16


def tables():
    at = np.arange(F, dtype=np.int64)
    k = at // 128 * 128 + -(at % 128 // FC) % 8 * FC + at % FC
    scale = 1.0 / (2.0 * math.sqrt(F * W * (ROUNDS * CB * CB * N_ROW * N_COL // NB)))
    weight = np.where(k == 0, 1.0, 2.0) * scale
    start = 128 * np.arange(8, dtype=np.int64) - LAGS // 2
    first = (start[:, None] * k[None, :] % NT) * (2.0 * np.pi / NT)
    cos1 = (np.cos(first) * weight).reshape(8, 2, HALF).transpose(1, 0, 2)
    sin1 = (np.sin(first) * weight).reshape(8, 2, HALF).transpose(1, 0, 2)
    e1 = np.stack([cos1, sin1], axis=1).astype(np.float32)
    second = (k[:, None] * np.arange(128, dtype=np.int64)[None, :] % NT) * (2.0 * np.pi / NT)
    cos2 = np.cos(second).reshape(2, HALF, 128)
    sin2 = -np.sin(second).reshape(2, HALF, 128)
    e2 = np.concatenate([cos2, sin2], axis=1).astype(np.float32)
    high = e2.astype(jnp.bfloat16)
    low = (e2 - high.astype(np.float32)).astype(jnp.bfloat16)
    return e1, np.stack([high, low], axis=0)


def flipper(value, bits):
    steps = [(1 << bit) * (1 - 2 * ((value // (1 << bit)) % 2)) for bit in range(bits)]

    def flip(mask):
        result = value
        for bit in range(bits):
            if mask >> bit & 1:
                result = result + steps[bit]
        return result

    return flip


def links(mask):
    steps = (0, 1, 2, 1)
    x, y, z = mask >> 2 & 3, mask >> 5 & 3, (mask >> 4 & 1) + (mask & 2)
    return steps[x] + steps[y] + steps[z]


def nt_dot(a, b):
    return lax.dot_general(a, b, (((1,), (1,)), ((), ())), preferred_element_type=F32)


def kernel(
    alive_hbm, spec_hbm, bins_hbm, e1_hbm, e2_hbm, out_ref,
    alive_ref, bins_ref, scale_v, x_v, d_v, send_v, recv_v, lhs_v, pbs_v, pbr_v, oh_v, cross_v, part0_v, part1_v, near0_v, near1_v, s2_v, r2_v, e1_v, e2_v,
    local_sem, pb_ss, pb_rs, a_ss, a_rs, f_ss, f_rs, near_ss, near_rs, far_ss, far_rs, entered,
):
    parts, nears = (part0_v, part1_v), (near0_v, near1_v)
    row = lax.axis_index("row")
    col = lax.axis_index("col")
    near = col // 4 * 2 + col % 2
    far = row * 2 + col // 2 % 2
    parity = (col + col // 2 + col // 4 + col // 8) % 2

    flip_row, flip_col, flip_near, flip_far = (
        flipper(value, bits) for value, bits in ((row, 3), (col, 4), (near, 3), (far, 4)))

    def device(mask):
        return (flip_row(mask >> 4), flip_col(mask & 15))

    loads = [
        pltpu.make_async_copy(source, target, local_sem.at[n])
        for n, (source, target) in enumerate([
            (bins_hbm, bins_ref), (alive_hbm, alive_ref), (spec_hbm, x_v), (e1_hbm, e1_v), (e2_hbm, e2_v)])
    ]
    for load in loads:
        load.start()

    peers = sorted([1, 4, 5, 8, 9, 12, 13, 2, 16, 18, 32, 64, 96], key=links, reverse=True)
    barrier = pltpu.get_barrier_semaphore()
    for mask in peers:
        pl.semaphore_signal(barrier, inc=1, device_id=device(mask), device_id_type=MESH)

    loads[0].wait()
    bins = bins_ref[...].reshape(ROUNDS * CB, CB)
    padded = jnp.concatenate([bins, jnp.zeros((128, 96), jnp.int32)], axis=1).astype(F32)
    pbs_v[...] = padded.T[:CB, :].astype(jnp.int32)
    loads[1].wait()
    loads[2].wait()

    def scales(i, _):
        x = x_v[i].astype(F32)
        power = jnp.mean(x * x, axis=-1, keepdims=True)
        alive = alive_ref[i].astype(F32)
        scale_v[i] = jnp.broadcast_to(alive / jnp.sqrt(power + 1e-06), (W, 128))
        return 0

    lax.fori_loop(0, CB, scales, 0, unroll=8)

    lane = lax.broadcasted_iota(jnp.int32, (8, 128), 1) // 16
    bits = [(lane // (1 << s)) % 2 == 1 for s in range(3)]

    def whiten(ft):
        def one(i, _):
            for c in range(2):
                at = pl.multiple_of(c * F + ft * 128, 128)
                t = x_v[i, :, pl.ds(at, 128)].astype(F32) * scale_v[i]
                t = pltpu.roll(t, 0, 1, stride=16, stride_axis=0)
                for s in range(3):
                    t = jnp.where(bits[s], pltpu.roll(t, 8 - (1 << s), 0), t)
                d_v[c, pl.ds(ft * 8 * CB + i, 8, stride=CB), :] = t
            return 0

        lax.fori_loop(0, CB, one, 0, unroll=8)

    def span(piece):
        return pl.ds(*SPANS[piece])

    def core_copy(piece):
        return pltpu.make_async_remote_copy(
            src_ref=send_v.at[span(piece)], dst_ref=recv_v.at[0, span(piece)],
            send_sem=a_ss.at[0, piece], recv_sem=a_rs.at[0, piece], device_id=device(1), device_id_type=MESH)

    def x_copy(piece):
        return pltpu.make_async_remote_copy(
            src_ref=send_v.at[span(piece)], dst_ref=recv_v.at[2, span(piece)],
            send_sem=a_ss.at[1, piece], recv_sem=a_rs.at[1, piece], device_id=device(4), device_id_type=MESH)

    def z_copy(piece):
        return pltpu.make_async_remote_copy(
            src_ref=send_v.at[span(piece)], dst_ref=recv_v.at[1, span(piece)],
            send_sem=a_ss.at[2, piece], recv_sem=a_rs.at[2, piece], device_id=device(2), device_id_type=MESH)

    def x_forward(piece):
        return pltpu.make_async_remote_copy(
            src_ref=recv_v.at[2, span(piece)], dst_ref=recv_v.at[3, span(piece)],
            send_sem=f_ss.at[piece], recv_sem=f_rs.at[piece], device_id=device(12), device_id_type=MESH)

    bin_copies = [
        pltpu.make_async_remote_copy(
            src_ref=pbs_v, dst_ref=pbr_v.at[r], send_sem=pb_ss.at[r], recv_sem=pb_rs.at[r],
            device_id=device(1 << r), device_id_type=MESH)
        for r in range(ROUNDS)
    ]

    def send(group, _):
        whiten((1 - parity) * GROUPS + group)

        def pack(k, _):
            q = group * 8 + k
            start = pl.multiple_of(((1 - parity) * CHUNKS + q) * CB, CB)
            for c in range(2):
                send_v[q, :, c * 128 : c * 128 + 128] = d_v[c, pl.ds(start, CB), :].astype(BF16)
            return 0

        lax.fori_loop(0, 8, pack, 0, unroll=2)

        if group == 0:
            pl.semaphore_wait(barrier, len(peers))
            for copy in bin_copies:
                copy.start()

        pieces = [k for k, (first, _) in enumerate(SPANS) if first // 8 == group]
        for piece in pieces:
            for make in (x_copy, z_copy, core_copy):
                make(piece).start()

        if group == 0:
            for along_z in (2, 16, 18):
                pl.semaphore_signal(entered, inc=1, device_id=device(along_z), device_id_type=MESH)
        return 0

    for group in range(GROUPS):
        send(group, 0)

    mask = (
        lax.broadcasted_iota(jnp.int32, (FC, 256), 1) % FC == lax.broadcasted_iota(jnp.int32, (FC, 256), 0)
    ).astype(F32).astype(BF16)

    def spread(q):
        start = (parity * CHUNKS + q) * CB
        for i in range(CB):
            v = [d_v[c, pl.ds(start + i, 8, stride=0), :] for c in range(2)]
            v = jnp.concatenate([jnp.concatenate([u, u], axis=0).astype(BF16) for u in v], axis=1)
            lhs_v[q, i * FC : i * FC + FC, :] = v * mask

    def rest(group, _):
        whiten(parity * GROUPS + group)

        def one(k, _):
            spread(group * 8 + k)
            return 0

        lax.fori_loop(0, 8, one, 0, unroll=2)
        return 0

    lax.fori_loop(0, GROUPS, rest, 0)

    def forward(piece):
        x_copy(piece).wait_recv()
        x_forward(piece).start()

    forward(0)
    forward(1)
    for copy in bin_copies:
        copy.wait()
    own = jnp.concatenate([bins_ref[r] for r in range(ROUNDS)], axis=1)
    of_round = lax.broadcasted_iota(jnp.int32, (CB, 128), 1) // CB
    other = pbr_v[0]
    for r in range(1, ROUNDS):
        other = jnp.where(of_round == r, pbr_v[r], other)
    place = lax.broadcasted_iota(jnp.int32, (NB, 128), 0)
    bin_ids = place // 2 % 8 * 16 + place // 32 * 4 + place % 2 * 2 + place // 16 % 2
    for i in range(CB):
        one = (own[i : i + 1, :] == bin_ids).astype(F32)
        two = (other[i : i + 1, :] == bin_ids).astype(F32)
        oh_v[0, :, i * 128 : i * 128 + 128] = (one + two).astype(BF16)
        oh_v[1, :, i * 128 : i * 128 + 128] = (one - two).astype(BF16)

    for k in range(2, LAG):
        forward(k)

    def products(q, _):
        other_part = recv_v[:, q].reshape(ROUNDS * CB, 256)
        turned = jnp.concatenate([-other_part[:, 128:], other_part[:, :128]], axis=1)
        rhs = jnp.concatenate([other_part, turned], axis=0)
        cross = nt_dot(lhs_v[q], rhs).astype(BF16)
        cross_v[:, pl.ds(pl.multiple_of(q * FC, FC), FC), :] = cross.reshape(CB, FC, 256)
        return 0

    near_mask = [k // 2 * 4 + k % 2 for k in range(NEAR)]
    far_mask = [k // 2 * 16 + k % 2 * 2 for k in range(FAR)]
    near_order = sorted(range(1, NEAR), key=lambda k: -links(near_mask[k]))
    far_order = sorted(range(1, FAR), key=lambda k: -links(far_mask[k]))

    def near_copy(g, k):
        return pltpu.make_async_remote_copy(
            src_ref=parts[g].at[flip_near(k)], dst_ref=nears[g].at[k - 1],
            send_sem=near_ss.at[g, k - 1], recv_sem=near_rs.at[g, k - 1],
            device_id=device(near_mask[k]), device_id_type=MESH)

    def stack(g):
        first, count = STACKS[g]
        for c in range(2):
            values = jnp.concatenate(
                [cross_v[i, first : first + count, c * 128 : c * 128 + 128] for i in range(CB)], axis=1)
            total = nt_dot(values, oh_v[c]).T
            parts[g][:, :, c * count : c * count + count] = total.astype(BF16).reshape(NEAR, FAR, count)
        for k in near_order:
            near_copy(g, k).start()

    for piece in range(LAG, PIECES + LAG):
        if piece < PIECES:
            forward(piece)
        before = piece - LAG
        core_copy(before).wait_recv()
        z_copy(before).wait_recv()
        x_forward(before).wait_recv()
        begin, number = SPANS[before]
        lax.fori_loop(0, number, lambda k, _: products(begin + k, _), 0, unroll=number)
        for g, (first, count) in enumerate(STACKS):
            if (begin + number) * FC == first + count:
                stack(g)

    def drain(piece, _):
        for make in (core_copy, x_copy, z_copy, x_forward):
            make(piece).wait_send()
        return 0

    for piece in range(PIECES):
        drain(piece, 0)

    for g, (first, count) in enumerate(STACKS):
        totals = [parts[g][near].astype(F32), None]
        for k in range(1, NEAR):
            near_copy(g, k).wait_recv()
            value = nears[g][k - 1].astype(F32)
            odd = bin(near_mask[k]).count("1") % 2
            totals[odd] = value if totals[odd] is None else totals[odd] + value
        for odd in range(2):
            half = parity if odd == 0 else 1 - parity
            for c in range(2):
                for n in range(count // 128):
                    at = half * 8 + c * GROUPS + first // 128 + n
                    value = totals[odd][:, c * count + n * 128 : c * count + n * 128 + 128]
                    s2_v[pl.ds(at, FAR, stride=16), :] = value

    far_copies = [
        pltpu.make_async_remote_copy(
            src_ref=s2_v.at[pl.ds(pl.multiple_of(flip_far(k) * 16, 16), 16), :], dst_ref=r2_v.at[k - 1],
            send_sem=far_ss.at[k - 1], recv_sem=far_rs.at[k - 1],
            device_id=device(far_mask[k]), device_id_type=MESH)
        for k in far_order
    ]
    pl.semaphore_wait(entered, 3)
    for copy in far_copies:
        copy.start()
    for g in range(len(STACKS)):
        for k in range(1, NEAR):
            near_copy(g, k).wait_send()
    loads[3].wait()
    loads[4].wait()
    sums = s2_v[pl.ds(pl.multiple_of(far * 16, 16), 16), :]
    for k, copy in zip(far_order, far_copies):
        copy.wait_recv()
        sums = sums + r2_v[k - 1]

    result = None
    for half in range(2):
        x = sums[half * 8 : half * 8 + 8]
        reals, imags = [], []
        for ft in range(3):
            cos1 = e1_v[half, 0, :, ft * 128 : ft * 128 + 128]
            sin1 = e1_v[half, 1, :, ft * 128 : ft * 128 + 128]
            re, im = x[ft : ft + 1, :], x[3 + ft : 4 + ft, :]
            reals.append(re * cos1 - im * sin1)
            imags.append(re * sin1 + im * cos1)
        turned = jnp.concatenate(reals + imags, axis=1)
        high = turned.astype(BF16)
        low = (turned - high.astype(F32)).astype(BF16)
        both = jnp.concatenate([high, low], axis=0)
        for part in range(2):
            o = jnp.dot(both, e2_v[part, half], preferred_element_type=F32)
            o = o[:8] + o[8:]
            result = o if result is None else result + o
    for mh in range(LAGS // 128):
        out_ref[0:1, mh * 128 : mh * 128 + 128] = result[mh : mh + 1, :]

    for copy in far_copies:
        copy.wait_send()


def on_device(spectra, pair_bins, dead_mask):
    e1, e2 = tables()
    dma = pltpu.SemaphoreType.DMA
    return pl.pallas_call(
        kernel,
        out_shape=jax.ShapeDtypeStruct((1, LAGS), F32),
        in_specs=[pl.BlockSpec(memory_space=pl.ANY)] * 5,
        out_specs=pl.BlockSpec(memory_space=pltpu.VMEM),
        scratch_shapes=[
            pltpu.SMEM((CB,), jnp.int32),
            pltpu.VMEM((ROUNDS, CB, CB), jnp.int32),
            pltpu.VMEM((CB, W, 128), F32),
            pltpu.VMEM((CB, W, 2 * F), BF16),
            pltpu.VMEM((2, 2 * CHUNKS * CB + 64, 128), F32),
            pltpu.VMEM((CHUNKS, CB, 256), BF16),
            pltpu.VMEM((ROUNDS, CHUNKS, CB, 256), BF16),
            pltpu.VMEM((CHUNKS, CB * FC, 256), BF16),
            pltpu.VMEM((CB, 128), jnp.int32),
            pltpu.VMEM((ROUNDS, CB, 128), jnp.int32),
            pltpu.VMEM((2, NB, CB * 128), BF16),
            pltpu.VMEM((CB, HALF, 256), BF16),
            *[pltpu.VMEM((NEAR, FAR, 2 * count), BF16) for _, count in STACKS],
            *[pltpu.VMEM((NEAR - 1, FAR, 2 * count), BF16) for _, count in STACKS],
            pltpu.VMEM((FAR * 16 + 16, 128), F32),
            pltpu.VMEM((FAR - 1, 16, 128), F32),
            pltpu.VMEM(e1.shape, F32),
            pltpu.VMEM(e2.shape, BF16),
            dma((5,)), dma((ROUNDS,)), dma((ROUNDS,)),
            dma((3, PIECES)), dma((3, PIECES)), dma((PIECES,)), dma((PIECES,)),
            dma((len(STACKS), NEAR - 1)), dma((len(STACKS), NEAR - 1)), dma((FAR - 1,)), dma((FAR - 1,)),
            pltpu.SemaphoreType.REGULAR,
        ],
        compiler_params=pltpu.CompilerParams(
            collective_id=0, has_side_effects=True, vmem_limit_bytes=48 << 20),
        name="correlate",
    )(*[
        pltpu.with_memory_space_constraint(x, pltpu.HBM)
        for x in (dead_mask, spectra, pair_bins, jnp.asarray(e1), jnp.asarray(e2))
    ])


def solution(mesh):
    return jax.shard_map(
        on_device,
        mesh=mesh,
        in_specs=(P(("row", "col"), None, None), P(None, ("row", "col"), None), P(("row", "col"))),
        out_specs=P(("row", "col"), None),
        check_vma=False,
    )
```
